256 devices in a mesh: front: 4 (over x), row: 8 (over z_hi, core), col: 8 (over y, z_lo).
Axes of the slice: x: 4, y: 4, z: 8 (z_hi: 4, z_lo: 2; z = z_hi * 2 + z_lo), core: 2. Of those that a mesh axis runs over, the one named last changes fastest.
Arguments:
- front: bfloat16 [4, 12288, 12288], P('front', 'row', 'col'), may hold values from -6 to 6
- panel: bfloat16 [4, 12288, 512], P('front', ('row', 'col')), may hold values from -8 to 8
- inverse: bfloat16 [4, 512, 512], P('front'), may hold values from -0.0046 to 0.056
- fill: int32 [4, 48], P('front'), may hold values 0 or 1
- block_map: int32 [4, 48], P('front'), may hold values from 0 to 47, as said below
- parent_front: bfloat16 [4, 6144, 12288], P('front', 'row', 'col'), may hold values from -6 to 6
Outputs:
- factor_rows: bfloat16 [4, 12288, 512], P('front', ('row', 'col'))
- parent: float32 [4, 6144, 12288], P('front', 'row', 'col')
The draws below stay inside these ranges and needn't reach their ends.
Inputs may be any that keep to these rules, and one draw needn't show every extreme that they name: `block_map`: each front's map is a permutation of its blocks that keeps every aligned group of 6 blocks in place as a group.
All inputs are finite; a program needn't handle non-finite values. No bound on the sum of `fill` on one device may be relied on, other than what follows from the above.
Results may differ from the reference program's by a relative error of at most 0.0025.
Values may be sent and summed in bfloat16 or wider, within the bound.
A program may use at most 64 MiB of HBM per device.

```python
import jax
import jax.numpy as jnp

M = 12288
PIVOTS = 512
BLK = 256
NF = 4
NBLK = 48
GRP = 6
TILE = 1536
HALF = 6144
N_ROW = 8


def draw_block_map(key, part):
    group_total = NBLK // GRP

    def one_front(front_key):
        group_keys = jax.random.split(front_key, group_total)
        orders = jax.vmap(lambda member_key: jax.random.permutation(member_key, GRP))(group_keys)
        shifted = orders + (jnp.arange(group_total, dtype=jnp.int32) * GRP)[:, None]
        return shifted.reshape(NBLK).astype(jnp.int32)
    return jax.vmap(one_front)(jax.random.split(key, NF))


def draw_inverse(key, part):
    diag_key, spread_key = jax.random.split(jax.random.fold_in(key, 7))
    diagonal = jax.random.uniform(diag_key, (NF, PIVOTS), jnp.float32, 0.035, 0.055)
    spread = jnp.clip(0.0013 * jax.random.normal(spread_key, (NF, PIVOTS, PIVOTS), jnp.float32), -0.0045, 0.0045)
    identity = jnp.eye(PIVOTS, dtype=jnp.float32)
    whole = spread * (1.0 - identity)[None] + diagonal[:, :, None] * identity[None]
    return whole.astype(jnp.bfloat16)


def touch_ends(drawn, rng, smallest, high):
    longest = drawn.shape.index(max(drawn.shape))
    spots = []
    for shift in (0, 1):
        where = [jax.random.randint(jax.random.fold_in(rng, axis), (), 0, length) for axis, length in enumerate(drawn.shape)]
        where[longest] = (where[longest] + shift) % drawn.shape[longest]
        spots.append(tuple(where))
    return drawn.at[spots[0]].set(smallest).at[spots[1]].set(high)


def level_of(key, dims, pieces, low, largest):
    def one(axis_at, shards_of):
        steps = jax.random.uniform(jax.random.fold_in(jax.random.fold_in(key, 6), axis_at), (shards_of,), jnp.float32, low / len(pieces), largest / len(pieces))
        return jnp.repeat(jnp.exp(steps), dims[axis_at] // shards_of).reshape((-1,) + (1,) * (len(dims) - axis_at - 1))

    loudness = one(*pieces[0])
    for cut in pieces[1:]:
        loudness = loudness * one(*cut)
    return loudness


def scatter_about(own_key, shape, scale, reach, pieces=(), kind=jnp.bfloat16):
    array = scale * jax.random.normal(own_key, shape, jnp.float32)
    if pieces:
        array = array * level_of(own_key, shape, pieces, -0.22, 0.18)
    return jnp.clip(array, -reach, reach).astype(kind)


def setup_inputs(seed: int = 0) -> dict:
    key_list = jax.random.split(jax.random.key(seed), 7)
    return {
        "front": scatter_about(key_list[0], (NF, M, M), 1.0, 6.0, ((0, 4), (1, 8), (2, 8))),
        "panel": scatter_about(key_list[1], (NF, M, PIVOTS), 2.5, 8.0, ((0, 4), (1, 64))),
        "inverse": draw_inverse(jax.random.fold_in(key_list[6], 71), 0),
        "fill": touch_ends((jax.random.randint(key_list[3], (NF, NBLK), 0, 3) < 2).astype(jnp.int32), jax.random.fold_in(key_list[3], 1), 0, 1),
        "block_map": draw_block_map(jax.random.fold_in(key_list[6], 71), 0),
        "parent_front": scatter_about(key_list[5], (NF, HALF, M), 1.0, 6.0, ((0, 4), (1, 8), (2, 8))),
    }


def block_inverse(mapping, block_total):
    target = jnp.arange(block_total, dtype=jnp.int32)
    matches = (mapping[:, None] == target[None, :]).astype(jnp.int32)
    return jnp.sum(matches * target[:, None], axis=0).astype(jnp.int32)


def reference(front, panel, inverse, fill, block_map, parent_front):
    factors = []
    contributions = []
    for member in range(NF):
        row_fill = jnp.repeat(fill[member], BLK).astype(jnp.bfloat16)
        masked = panel[member] * row_fill[:, None]
        factor = jnp.dot(masked, jnp.triu(inverse[member]), preferred_element_type=jnp.float32).astype(jnp.bfloat16)
        factors.append(factor)
        schur = front[member].astype(jnp.float32) - jnp.dot(factor, factor.T, preferred_element_type=jnp.float32)
        source = block_inverse(block_map[member], NBLK)
        blocked = jnp.take(schur.reshape(NBLK, BLK, NBLK, BLK), source, axis=0)
        blocked = jnp.take(blocked, source, axis=2)
        contributions.append(blocked.reshape(M, M).astype(jnp.bfloat16))
    halves = []
    for member in range(NF):
        paired = member // 2 * 2
        summed = contributions[paired].astype(jnp.float32) + contributions[paired + 1].astype(jnp.float32)
        layout = summed.reshape(N_ROW, 2, TILE // 2, M)[:, member % 2].reshape(HALF, M)
        halves.append(parent_front[member].astype(jnp.float32) + layout)
    return jnp.stack(factors), jnp.stack(halves)
```

```python
import jax
import jax.numpy as jnp
from jax import lax
from jax.experimental import pallas as pl
from jax.experimental.pallas import tpu as pltpu
from jax.sharding import PartitionSpec as P

BLK = 256
MESH = pl.DeviceIdType.MESH


def local_source(map_ref, base, target, count):
    found = jnp.int32(0)
    for i in range(count):
        found = found + jnp.where(map_ref[0, base + i] == base + target, i, 0)
    return found


def prologue_kernel(map_ref, fill_ref, panel_ref, inverse_ref, front_ref, factor_ref, sent_ref, sems):
    row = lax.axis_index("row")
    col = lax.axis_index("col")
    parity = lax.axis_index("front") % 2
    per_tile = front_ref.shape[0]
    half = per_tile // 2
    copies = []
    for i in range(half):
        block = local_source(map_ref, row * per_tile, (1 - parity) * half + i, per_tile)
        copy = pltpu.make_async_copy(front_ref.at[block], sent_ref.at[i], sems.at[i])
        copy.start()
        copies.append(copy)
    size = inverse_ref.shape[0]
    upper = lax.broadcasted_iota(jnp.int32, (size, size), 0) <= lax.broadcasted_iota(
        jnp.int32, (size, size), 1
    )
    inverse = jnp.where(upper, inverse_ref[...].astype(jnp.float32), 0.0).astype(jnp.bfloat16)
    local_rows = panel_ref.shape[0]
    piece = 64
    shard = row * lax.axis_size("col") + col
    for t in range(local_rows // piece):
        block = (shard * local_rows + t * piece) // BLK
        keep = fill_ref[0, block].astype(jnp.float32)
        masked = (panel_ref[t * piece:(t + 1) * piece, :].astype(jnp.float32) * keep).astype(jnp.bfloat16)
        factor_ref[t * piece:(t + 1) * piece, :] = jnp.dot(
            masked, inverse, preferred_element_type=jnp.float32
        ).astype(jnp.bfloat16)
    for copy in copies:
        copy.wait()


def prologue(block_map, fill, panel, inverse, front_blocks):
    half = front_blocks.shape[0] // 2
    return pl.pallas_call(
        prologue_kernel,
        out_shape=(
            jax.ShapeDtypeStruct(panel.shape, jnp.bfloat16),
            jax.ShapeDtypeStruct((half,) + front_blocks.shape[1:], jnp.bfloat16),
        ),
        in_specs=[
            pl.BlockSpec(memory_space=pltpu.SMEM),
            pl.BlockSpec(memory_space=pltpu.SMEM),
            pl.BlockSpec(memory_space=pltpu.VMEM),
            pl.BlockSpec(memory_space=pltpu.VMEM),
            pl.BlockSpec(memory_space=pl.ANY),
        ],
        out_specs=(pl.BlockSpec(memory_space=pltpu.VMEM), pl.BlockSpec(memory_space=pl.ANY)),
        scratch_shapes=[pltpu.SemaphoreType.DMA((half,))],
        name="prologue",
    )(block_map, fill, panel, inverse, front_blocks)


def gather_kernel(own_ref, out_ref, local_sem, x_sem, row_recv, col_recv, row_send, chain_send, twin_send):
    front = lax.axis_index("front")
    row = lax.axis_index("row")
    col = lax.axis_index("col")
    zh, core = row // 2, row % 2
    y, zl = col // 2, col % 2
    partner = front + 1 - 2 * (front % 2)

    def device(f=None, zh_=None, core_=None, y_=None, zl_=None):
        return {
            "front": front if f is None else f,
            "row": (zh if zh_ is None else zh_) * 2 + (core if core_ is None else core_),
            "col": (y if y_ is None else y_) * 2 + (zl if zl_ is None else zl_),
        }

    y_up, y_down = (y + 1) % 4, (y + 3) % 4
    z_up, z_down = (zh + 1) % 4, (zh + 3) % 4

    barrier = pltpu.get_barrier_semaphore()
    peers = [
        device(f=partner),
        device(zl_=1 - zl),
        device(y_=y_up),
        device(y_=y_down),
        device(core_=1 - core),
    ]
    for other in (z_up, z_down):
        for k in range(2):
            peers.append(device(zh_=other, core_=k))
    for peer in peers:
        pl.semaphore_signal(barrier, inc=1, device_id=peer, device_id_type=MESH)
    pl.semaphore_wait(barrier, len(peers))

    distance = (zh - y + 4 + core * 2 * (y - zh)) % 4
    late = (core + zl) % 2
    step_of = distance + late
    at_home = zh == y
    is_source = jnp.logical_and(at_home, core == zl)
    is_twin = jnp.logical_and(at_home, core != zl)
    chained = jnp.logical_not(at_home)
    next_zh = (zh + 1 + 2 * core) % 4
    me = y * 2 + zl
    started = []

    def remote(cond, src, dst, send, recv, target):
        copy = pltpu.make_async_remote_copy(
            src_ref=src, dst_ref=dst, send_sem=send, recv_sem=recv, device_id=target, device_id_type=MESH
        )
        if cond is None:
            copy.start()
        else:
            pl.when(cond)(copy.start)
        started.append((cond, copy))

    def arrived(e, kind, j):
        sem = (row_recv if kind == 0 else col_recv).at[e, j]
        there = out_ref.at[2 * kind + e, j]
        pltpu.make_async_copy(there, there, sem).wait()

    def row_slot(e, j):
        return own_ref if (e == 0 and j is me) else out_ref.at[e, j]

    def send_row(e, n, j, target):
        remote(None, row_slot(e, j), out_ref.at[e, j], row_send.at[e, n], row_recv.at[e, j], target)

    def start_chain(e, j, zl_of):
        remote(
            is_source, row_slot(e, j), out_ref.at[2 + e, j], chain_send.at[e, j], col_recv.at[e, j],
            device(zh_=(zh + 1 + 2 * zl_of) % 4, core_=zl_of),
        )
        remote(
            is_source, row_slot(e, j), out_ref.at[2 + e, j], twin_send.at[e, j], col_recv.at[e, j],
            device(core_=1 - core),
        )

    def pass_chain(e, stage, n):
        if not 0 <= n - stage:
            return
        offsets = ((0,), (3, 1), (2,))[stage]
        here = jnp.logical_and(chained, step_of == n - stage)
        onward = jnp.logical_and(here, distance < 3)
        for dy in offsets:
            j = ((y + dy) % 4) * 2 + core
            pl.when(here)(lambda: arrived(e, 1, j))
            remote(
                onward, out_ref.at[2 + e, j], out_ref.at[2 + e, j], chain_send.at[e, j], col_recv.at[e, j],
                device(zh_=next_zh),
            )
            remote(
                here, out_ref.at[2 + e, j], out_ref.at[2 + e, j], twin_send.at[e, j], col_recv.at[e, j],
                device(core_=1 - core),
            )

    def level(e, n):
        other = 1 - zl
        if n == 0:
            if e == 1:
                arrived(1, 0, me)
            send_row(e, 0, me, device(zl_=other))
            send_row(e, 1, me, device(y_=y_up))
            send_row(e, 2, me, device(y_=y_down))
            start_chain(e, me, zl)
        if n == 1:
            j = y * 2 + other
            arrived(e, 0, j)
            send_row(e, 3, j, device(y_=y_up))
            send_row(e, 4, j, device(y_=y_down))
            start_chain(e, j, other)
        if n in (1, 2):
            side = zl if n == 1 else other
            down = y_down * 2 + side
            up = y_up * 2 + side
            arrived(e, 0, down)
            arrived(e, 0, up)
            send_row(e, 4 + n, ((y + 3 + 2 * side) % 4) * 2 + side, device(y_=(y + 1 + 2 * side) % 4))
            start_chain(e, down, side)
            start_chain(e, up, side)
        if n in (2, 3):
            side = zl if n == 2 else other
            far = ((y + 2) % 4) * 2 + side
            arrived(e, 0, far)
            start_chain(e, far, side)
        if n >= 1:
            for stage in range(3):
                if 1 <= n - stage <= 4:
                    pass_chain(e, stage, n)

    keep = pltpu.make_async_copy(own_ref, out_ref.at[0, me], local_sem)
    keep.start()
    remote(None, own_ref, out_ref.at[1, me], x_sem, row_recv.at[1, me], device(f=partner))
    lag = 2
    for g in range(7 + lag):
        if g < 7:
            level(0, g)
        if 0 <= g - lag:
            level(1, g - lag)

    for e in range(2):
        for j in range(8):
            pl.when(is_twin)(lambda: arrived(e, 1, jnp.int32(j)))
        for dy in range(4):
            pl.when(chained)(lambda: arrived(e, 1, ((y + dy) % 4) * 2 + (1 - core)))
    keep.wait()
    for cond, copy in started:
        if cond is None:
            copy.wait_send()
        else:
            pl.when(cond)(copy.wait_send)


def gather(factor):
    rows, depth = factor.shape
    return pl.pallas_call(
        gather_kernel,
        out_shape=jax.ShapeDtypeStruct((4, 8, rows, depth), jnp.bfloat16),
        in_specs=[pl.BlockSpec(memory_space=pl.ANY)],
        out_specs=pl.BlockSpec(memory_space=pl.ANY),
        scratch_shapes=[
            pltpu.SemaphoreType.DMA,
            pltpu.SemaphoreType.DMA,
            pltpu.SemaphoreType.DMA((2, 8)),
            pltpu.SemaphoreType.DMA((2, 8)),
            pltpu.SemaphoreType.DMA((2, 7)),
            pltpu.SemaphoreType.DMA((2, 8)),
            pltpu.SemaphoreType.DMA((2, 8)),
        ],
        compiler_params=pltpu.CompilerParams(collective_id=0, has_side_effects=True),
        cost_estimate=pl.CostEstimate(flops=0, bytes_accessed=150_000_000, transcendentals=0),
        name="gather",
    )(factor)


def finish_kernel(idx_ref, front_ref, came_ref, own_row_ref, far_row_ref, own_col_ref, far_col_ref, parent_ref, out_ref):
    contract = (((1,), (1,)), ((), ()))
    own_rows = own_row_ref[...]
    far_rows = far_row_ref[...]
    for b in range(6):
        own = pl.ds(pl.multiple_of(idx_ref[6 + b] * BLK, BLK), BLK)
        far = pl.ds(pl.multiple_of(idx_ref[12 + b] * BLK, BLK), BLK)
        here = slice(b * BLK, (b + 1) * BLK)
        update = lax.dot_general(own_rows, own_col_ref[own, :], contract, preferred_element_type=jnp.float32)
        mine = (front_ref[:, own].astype(jnp.float32) - update).astype(jnp.bfloat16)
        update = lax.dot_general(far_rows, far_col_ref[far, :], contract, preferred_element_type=jnp.float32)
        theirs = (came_ref[:, far].astype(jnp.float32) - update).astype(jnp.bfloat16)
        out_ref[:, here] = parent_ref[:, here].astype(jnp.float32) + (
            mine.astype(jnp.float32) + theirs.astype(jnp.float32)
        )


def finish(idx, front, came, factors, parent_front):
    tile = front.shape[1]
    depth = factors.shape[2]
    half = parent_front.shape[0]
    spec = pltpu.PrefetchScalarGridSpec(
        num_scalar_prefetch=1,
        grid=(half // BLK,),
        in_specs=[
            pl.BlockSpec((BLK, tile), lambda a, idx: (idx[a], 0)),
            pl.BlockSpec((BLK, tile), lambda a, idx: (a, 0)),
            pl.BlockSpec((None, BLK, depth), lambda a, idx: (0, idx[a], 0)),
            pl.BlockSpec((None, BLK, depth), lambda a, idx: (1, idx[3 + a], 0)),
            pl.BlockSpec((None, tile, depth), lambda a, idx: (idx[18], 0, 0)),
            pl.BlockSpec((None, tile, depth), lambda a, idx: (idx[18] + 1, 0, 0)),
            pl.BlockSpec((BLK, tile), lambda a, idx: (a, 0)),
        ],
        out_specs=pl.BlockSpec((BLK, tile), lambda a, idx: (a, 0)),
    )
    return pl.pallas_call(
        finish_kernel,
        grid_spec=spec,
        out_shape=jax.ShapeDtypeStruct((half, tile), jnp.float32),
        compiler_params=pltpu.CompilerParams(vmem_limit_bytes=40 * 2**20),
        cost_estimate=pl.CostEstimate(flops=4 * half * tile * depth, bytes_accessed=20_000_000, transcendentals=0),
        name="finish",
    )(idx, front, came, factors, factors, factors, factors, parent_front)


def swap_pairs(block, axis):
    count = lax.axis_size(axis)
    return lax.ppermute(block, axis, [(i, i ^ 1) for i in range(count)])


def group_source(mapping, start, count):
    group = lax.dynamic_slice_in_dim(mapping, start, count, 0) - start
    target = jnp.arange(count, dtype=jnp.int32)
    return jnp.sum((group[:, None] == target[None, :]).astype(jnp.int32) * target[:, None], axis=0)


def shards(front, panel, inverse, fill, block_map, parent_front):
    row = lax.axis_index("row")
    col = lax.axis_index("col")
    parity = lax.axis_index("front") % 2
    tile = front.shape[1]
    per_tile = tile // BLK
    half = per_tile // 2
    far_map = swap_pairs(block_map[0], "front")
    factor, sent = prologue(block_map, fill, panel[0], inverse[0], front.reshape(per_tile, BLK, tile))
    came = swap_pairs(sent, "front")
    gathered = gather(factor).reshape(4, tile, factor.shape[1])
    picks = [
        lax.dynamic_slice_in_dim(group_source(m, row * per_tile, per_tile), parity * half, half, 0)
        for m in (block_map[0], far_map)
    ]
    picks += [group_source(m, col * per_tile, per_tile) for m in (block_map[0], far_map)]
    home = jnp.logical_and(row // 2 == col // 2, row % 2 == col % 2)
    picks.append(jnp.where(home, 0, 2).astype(jnp.int32)[None])
    idx = jnp.concatenate(picks)
    parent = finish(idx, front[0], came.reshape(half * BLK, tile), gathered, parent_front[0])
    return (factor[None], parent[None])


def solution(mesh):
    placed = (
        P("front", "row", "col"),
        P("front", ("row", "col"), None),
        P("front", None, None),
        P("front", None),
        P("front", None),
        P("front", "row", "col"),
    )
    return jax.shard_map(
        shards,
        mesh=mesh,
        in_specs=placed,
        out_specs=(P("front", ("row", "col"), None), P("front", "row", "col")),
        check_vma=False,
    )
```

```python
import jax
import jax.numpy as jnp
from jax import lax
from jax.experimental import pallas as pl
from jax.experimental.pallas import tpu as pltpu
from jax.sharding import PartitionSpec as P

BLK = 256
MESH = pl.DeviceIdType.MESH


def local_source(map_ref, base, target, count):
    found = jnp.int32(0)
    for i in range(count):
        found = found + jnp.where(map_ref[0, base + i] == base + target, i, 0)
    return jnp.clip(found, 0, count - 1)


def kernel(
    map_ref, fill_ref, map_any, panel_any, inverse_any, front_any, parent_any,
    factor_ref, base,
    tiles, front_v, sent, came, update, parent_v, panel_v, inverse_v, far_v, far_map,
    load_sem, far_sem, map_sems, x_sem, front_send, front_recv,
    row_recv, col_recv, row_send, chain_send, twin_send,
):
    front = lax.axis_index("front")
    row = lax.axis_index("row")
    col = lax.axis_index("col")
    zh, core = row // 2, row % 2
    y, zl = col // 2, col % 2
    parity = front % 2
    partner = front + 1 - 2 * parity
    per_tile = front_v.shape[0]
    half = per_tile // 2
    local_rows = panel_v.shape[0]
    fine = tiles.shape[2]
    pieces = local_rows // fine
    per_block = BLK // fine

    def device(f=None, zh_=None, core_=None, y_=None, zl_=None):
        return {
            "front": front if f is None else f,
            "row": (zh if zh_ is None else zh_) * 2 + (core if core_ is None else core_),
            "col": (y if y_ is None else y_) * 2 + (zl if zl_ is None else zl_),
        }

    barrier = pltpu.get_barrier_semaphore()
    peers = [device(f=partner), device(zl_=1 - zl), device(core_=1 - core)]
    peers += [device(y_=(y + n) % 4) for n in (1, 3)]
    peers += [device(zh_=(zh + n) % 4, core_=k) for n in (1, 3) for k in range(2)]
    for peer in peers:
        pl.semaphore_signal(barrier, inc=1, device_id=peer, device_id_type=MESH)

    loads = [
        pltpu.make_async_copy(panel_any, panel_v, load_sem.at[0]),
        pltpu.make_async_copy(inverse_any, inverse_v, load_sem.at[1]),
        pltpu.make_async_copy(parent_any, parent_v, load_sem.at[2]),
    ] + [
        pltpu.make_async_copy(front_any.at[:, :, pl.ds(b * BLK, BLK)], front_v.at[:, b], load_sem.at[3 + b])
        for b in range(per_tile)
    ]
    for load in loads:
        load.start()

    at_home = zh == y
    is_source = jnp.logical_and(at_home, core == zl)
    is_twin = jnp.logical_and(at_home, core != zl)
    chained = jnp.logical_not(at_home)
    distance = (zh - y + 4 + core * 2 * (y - zh)) % 4
    onward = jnp.logical_and(chained, distance < 3)
    next_zh = (zh + 1 + 2 * core) % 4
    other = 1 - zl
    me = y * 2 + zl
    across = y * 2 + other

    def slot(kind, j):
        return tiles.at[kind, pl.ds(j * pieces, pieces)]

    loads[0].wait()
    loads[1].wait()
    size = inverse_v.shape[0]
    upper = lax.broadcasted_iota(jnp.int32, (size, size), 0) <= lax.broadcasted_iota(
        jnp.int32, (size, size), 1
    )
    inverse = jnp.where(upper, inverse_v[...].astype(jnp.float32), 0.0).astype(jnp.bfloat16)
    piece = 64
    shard = row * lax.axis_size("col") + col
    for t in range(local_rows // piece):
        block = (shard * local_rows + t * piece) // BLK
        keep = fill_ref[0, block].astype(jnp.float32)
        masked = (panel_v[t * piece:(t + 1) * piece, :].astype(jnp.float32) * keep).astype(jnp.bfloat16)
        rows = jnp.dot(masked, inverse, preferred_element_type=jnp.float32).astype(jnp.bfloat16)
        factor_ref[t * piece:(t + 1) * piece, :] = rows
        for q in range(piece // fine):
            tiles[0, me * pieces + t * (piece // fine) + q] = rows[q * fine:(q + 1) * fine]

    row_first = row * per_tile
    col_first = col * per_tile
    for load in loads[3:]:
        load.wait()
    for i in range(half):
        block = local_source(map_ref, row_first, (1 - parity) * half + i, per_tile)
        for b in range(per_tile):
            sent[i, b] = front_v[block, local_source(map_ref, col_first, b, per_tile)]

    pl.semaphore_wait(barrier, len(peers))

    started = []

    def remote(cond, src, dst, send, recv, target):
        copy = pltpu.make_async_remote_copy(
            src_ref=src, dst_ref=dst, send_sem=send, recv_sem=recv, device_id=target, device_id_type=MESH
        )
        if cond is None:
            copy.start()
        else:
            pl.when(cond)(copy.start)
        started.append((cond, copy))
        return copy

    parts = 2

    def part(kind, j, h):
        return tiles.at[kind, pl.ds(j * pieces + h * (pieces // parts), pieces // parts)]

    def arrived(e, kind, j):
        sem = row_recv.at[e, j] if kind == 0 else col_recv.at[e, j, 0]
        there = slot(2 * kind + e, j)
        pltpu.make_async_copy(there, there, sem).wait()

    def spread(e, n, j, target):
        remote(None, slot(e, j), slot(e, j), row_send.at[e, n], row_recv.at[e, j], target)

    def own(e):
        spread(e, 0, me, device(zl_=other))
        spread(e, 1, me, device(y_=(y + 1) % 4))
        spread(e, 2, me, device(y_=(y + 3) % 4))
        start_chain(e, me, True)

    def cross(e):
        arrived(e, 0, across)
        spread(e, 3, across, device(y_=(y + 1) % 4))
        spread(e, 4, across, device(y_=(y + 3) % 4))
        start_chain(e, across, False)

    def relay(e, near):
        side = zl if near else other
        down = ((y + 3) % 4) * 2 + side
        up = ((y + 1) % 4) * 2 + side
        arrived(e, 0, down)
        arrived(e, 0, up)
        spread(
            e, 5 if near else 6, ((y + 3 + 2 * side) % 4) * 2 + side, device(y_=(y + 1 + 2 * side) % 4)
        )
        start_chain(e, down, near)
        start_chain(e, up, near)

    def last(e, near):
        j = ((y + 2) % 4) * 2 + (zl if near else other)
        pl.when(is_source)(lambda: arrived(e, 0, j))
        start_chain(e, j, near)

    in_flight = {}

    def start_chain(e, j, near):
        side = zl if near else other
        for h in range(parts):
            if (near, h) in in_flight:
                before = in_flight[near, h]
                pl.when(is_source)(before.wait_send)
                started[:] = [item for item in started if item[1] is not before]
            in_flight[near, h] = remote(
                is_source, part(e, j, h), part(2 + e, j, h), chain_send.at[e, j, h], col_recv.at[e, j, h],
                device(zh_=(zh + 1 + 2 * side) % 4, core_=side),
            )
        remote(
            is_source, slot(e, j), slot(2 + e, j), twin_send.at[e, j], col_recv.at[e, j, 0], device(core_=1 - core)
        )

    def pass_chain(e, dy):
        j = ((y + dy) % 4) * 2 + core
        for h in range(parts):
            here = part(2 + e, j, h)
            pl.when(chained)(pltpu.make_async_copy(here, here, col_recv.at[e, j, h]).wait)
            remote(onward, here, here, chain_send.at[e, j, h], col_recv.at[e, j, h], device(zh_=next_zh))
        here = slot(2 + e, j)
        remote(chained, here, here, twin_send.at[e, j], col_recv.at[e, j, 0], device(core_=1 - core))

    tell = pltpu.make_async_remote_copy(
        src_ref=map_any, dst_ref=far_v, send_sem=map_sems.at[0], recv_sem=map_sems.at[1],
        device_id=device(f=partner), device_id_type=MESH,
    )
    tell.start()
    exchange = pltpu.make_async_remote_copy(
        src_ref=slot(0, me), dst_ref=slot(1, me), send_sem=x_sem, recv_sem=row_recv.at[1, me],
        device_id=device(f=partner), device_id_type=MESH,
    )
    exchange.start()
    fronts = []
    for i in range(half):
        fronts.append(pltpu.make_async_remote_copy(
            src_ref=sent.at[i], dst_ref=came.at[i], send_sem=front_send.at[i],
            recv_sem=front_recv.at[i], device_id=device(f=partner), device_id_type=MESH,
        ))
        fronts[i].start()

    own(0)
    cross(0)
    relay(0, True)
    arrived(1, 0, me)
    own(1)
    relay(0, False)
    pass_chain(0, 0)
    cross(1)
    last(0, True)
    pass_chain(0, 3)
    relay(1, True)
    last(0, False)
    pass_chain(0, 1)
    pass_chain(0, 2)
    relay(1, False)
    pass_chain(1, 0)
    last(1, True)
    last(1, False)
    for dy in (3, 1, 2):
        pass_chain(1, dy)

    tell.wait()
    far_copy = pltpu.make_async_copy(far_v, far_map, far_sem)
    far_copy.start()
    far_copy.wait()
    exchange.wait_send()
    for e in range(2):
        for j in range(8):
            pl.when(is_twin)(lambda: arrived(e, 1, jnp.int32(j)))
        for dy in range(4):
            pl.when(chained)(lambda: arrived(e, 1, ((y + dy) % 4) * 2 + (1 - core)))
        for side in range(2):
            pl.when(jnp.logical_not(is_source))(lambda: arrived(e, 0, ((y + 2) % 4) * 2 + side))

    loads[2].wait()
    col_kind = jnp.where(is_source, 0, 2)
    contract = (((1,), (1,)), ((), ()))

    def take(kind, block):
        return jnp.concatenate([tiles[kind, block * per_block + q] for q in range(per_block)], axis=0)

    def products(e, maps, use):
        for a in range(half):
            block = local_source(maps, row_first, parity * half + a, per_tile)
            rows = take(e, block)
            for b in range(per_tile):
                source = local_source(maps, col_first, b, per_tile)
                cols = take(col_kind + e, source)
                use(a, b, block, source, lax.dot_general(rows, cols, contract, preferred_element_type=jnp.float32))

    def use_own(a, b, block, source, product):
        entries = front_v[block, source]
        mine = (entries.astype(jnp.float32) - product).astype(jnp.bfloat16).astype(jnp.float32)
        base[a, :, b * BLK:(b + 1) * BLK] = parent_v[a, :, b * BLK:(b + 1) * BLK].astype(jnp.float32) + mine

    def use_far(a, b, block, source, product):
        update[a, :, b * BLK:(b + 1) * BLK] = product

    products(0, map_ref, use_own)
    products(1, far_map, use_far)

    for a in range(half):
        fronts[a].wait()
        for b in range(per_tile):
            entries = came[a, b]
            where = slice(b * BLK, (b + 1) * BLK)
            theirs = (entries.astype(jnp.float32) - update[a, :, where]).astype(jnp.bfloat16)
            base[a, :, where] = base[a, :, where] + theirs.astype(jnp.float32)
    for cond, copy in started:
        if cond is None:
            copy.wait_send()
        else:
            pl.when(cond)(copy.wait_send)


def shards(front, panel, inverse, fill, block_map, parent_front):
    tile = front.shape[1]
    per_tile = tile // BLK
    half = per_tile // 2
    local_rows, depth = panel.shape[1:]
    anywhere = pl.BlockSpec(memory_space=pl.ANY)
    dma = pltpu.SemaphoreType.DMA
    bf16, f32 = jnp.bfloat16, jnp.float32
    factor, parent = pl.pallas_call(
        kernel,
        out_shape=(
            jax.ShapeDtypeStruct((local_rows, depth), bf16),
            pltpu.VMEM((half, BLK, tile), f32),
        ),
        in_specs=[pl.BlockSpec(memory_space=pltpu.SMEM)] * 2 + [anywhere] * 5,
        out_specs=(pl.BlockSpec(memory_space=pltpu.VMEM), pl.BlockSpec(memory_space=pltpu.VMEM)),
        scratch_shapes=[
            pltpu.VMEM((4, tile // 32, 32, depth), bf16),
            pltpu.VMEM((per_tile, per_tile, BLK, BLK), bf16),
            pltpu.VMEM((half, per_tile, BLK, BLK), bf16),
            pltpu.VMEM((half, per_tile, BLK, BLK), bf16),
            pltpu.VMEM((half, BLK, tile), f32),
            pltpu.VMEM((half, BLK, tile), bf16),
            pltpu.VMEM((local_rows, depth), bf16),
            pltpu.VMEM((depth, depth), bf16),
            pltpu.VMEM(block_map.shape, jnp.int32),
            pltpu.SMEM(block_map.shape, jnp.int32),
            dma((3 + per_tile,)), dma, dma((2,)), dma, dma((half,)), dma((half,)),
            dma((2, 8)), dma((2, 8, 2)), dma((2, 7)), dma((2, 8, 2)), dma((2, 8)),
        ],
        compiler_params=pltpu.CompilerParams(
            collective_id=0, has_side_effects=True, vmem_limit_bytes=56 * 2**20
        ),
        name="panel_and_extend_add",
    )(
        block_map, fill, block_map, panel[0], inverse[0], front.reshape(per_tile, BLK, tile),
        parent_front.reshape(half, BLK, tile),
    )
    return (factor[None], parent.reshape(1, half * BLK, tile))


def solution(mesh):
    placed = (
        P("front", "row", "col"),
        P("front", ("row", "col"), None),
        P("front", None, None),
        P("front", None),
        P("front", None),
        P("front", "row", "col"),
    )
    return jax.shard_map(
        shards,
        mesh=mesh,
        in_specs=placed,
        out_specs=(P("front", ("row", "col"), None), P("front", "row", "col")),
        check_vma=False,
    )
```

```python
import jax
import jax.numpy as jnp
from jax import lax
from jax.experimental import pallas as pl
from jax.experimental.pallas import tpu as pltpu
from jax.sharding import PartitionSpec as P

BLK = 256
MESH = pl.DeviceIdType.MESH


def local_source(map_ref, base, target, count):
    found = jnp.int32(0)
    for i in range(count):
        found = found + jnp.where(map_ref[0, base + i] == base + target, i, 0)
    return jnp.clip(found, 0, count - 1)


def kernel(
    map_ref, fill_ref, map_any, panel_any, inverse_any, front_any, parent_any,
    factor_ref, base,
    own_tiles, far_tiles, front_v, sent, came, parent_v, panel_v, inverse_v, far_v, far_map,
    load_sem, far_sem, map_sems, x_sem, front_send, front_recv,
    row_recv, col_recv, row_send, chain_send, twin_send,
):
    front = lax.axis_index("front")
    row = lax.axis_index("row")
    col = lax.axis_index("col")
    zh, core = row // 2, row % 2
    y, zl = col // 2, col % 2
    parity = front % 2
    partner = front + 1 - 2 * parity
    per_tile = front_v.shape[0]
    half = per_tile // 2
    local_rows = panel_v.shape[0]
    tiles = (own_tiles, far_tiles)
    fine = own_tiles.shape[2]
    pieces = local_rows // fine
    per_block = BLK // fine

    def device(f=None, zh_=None, core_=None, y_=None, zl_=None):
        return {
            "front": front if f is None else f,
            "row": (zh if zh_ is None else zh_) * 2 + (core if core_ is None else core_),
            "col": (y if y_ is None else y_) * 2 + (zl if zl_ is None else zl_),
        }

    barrier = pltpu.get_barrier_semaphore()
    peers = [device(f=partner), device(zl_=1 - zl), device(core_=1 - core)]
    peers += [device(y_=(y + n) % 4) for n in (1, 3)]
    peers += [device(zh_=(zh + n) % 4, core_=k) for n in (1, 3) for k in range(2)]
    for peer in peers:
        pl.semaphore_signal(barrier, inc=1, device_id=peer, device_id_type=MESH)

    loads = [
        pltpu.make_async_copy(panel_any, panel_v, load_sem.at[0]),
        pltpu.make_async_copy(inverse_any, inverse_v, load_sem.at[1]),
        pltpu.make_async_copy(parent_any, parent_v, load_sem.at[2]),
    ] + [
        pltpu.make_async_copy(front_any.at[:, :, pl.ds(b * BLK, BLK)], front_v.at[:, b], load_sem.at[3 + b])
        for b in range(per_tile)
    ]
    for load in loads:
        load.start()

    at_home = zh == y
    is_source = jnp.logical_and(at_home, core == zl)
    is_twin = jnp.logical_and(at_home, core != zl)
    chained = jnp.logical_not(at_home)
    distance = (zh - y + 4 + core * 2 * (y - zh)) % 4
    onward = jnp.logical_and(chained, distance < 3)
    next_zh = (zh + 1 + 2 * core) % 4
    other = 1 - zl
    me = y * 2 + zl
    across = y * 2 + other

    def slot(kind, j):
        return tiles[kind % 2].at[kind // 2, pl.ds(j * pieces, pieces)]

    loads[0].wait()
    loads[1].wait()
    size = inverse_v.shape[0]
    upper = lax.broadcasted_iota(jnp.int32, (size, size), 0) <= lax.broadcasted_iota(
        jnp.int32, (size, size), 1
    )
    inverse = jnp.where(upper, inverse_v[...].astype(jnp.float32), 0.0).astype(jnp.bfloat16)
    piece = 64
    shard = row * lax.axis_size("col") + col
    for t in range(local_rows // piece):
        block = (shard * local_rows + t * piece) // BLK
        keep = fill_ref[0, block].astype(jnp.float32)
        masked = (panel_v[t * piece:(t + 1) * piece, :].astype(jnp.float32) * keep).astype(jnp.bfloat16)
        rows = jnp.dot(masked, inverse, preferred_element_type=jnp.float32).astype(jnp.bfloat16)
        factor_ref[t * piece:(t + 1) * piece, :] = rows
        for q in range(piece // fine):
            own_tiles[0, me * pieces + t * (piece // fine) + q] = rows[q * fine:(q + 1) * fine]

    row_first = row * per_tile
    col_first = col * per_tile
    for load in loads[3:]:
        load.wait()
    for i in range(half):
        block = local_source(map_ref, row_first, (1 - parity) * half + i, per_tile)
        for b in range(per_tile):
            sent[i, b] = front_v[block, local_source(map_ref, col_first, b, per_tile)]

    pl.semaphore_wait(barrier, len(peers))

    started = []

    def remote(cond, src, dst, send, recv, target):
        copy = pltpu.make_async_remote_copy(
            src_ref=src, dst_ref=dst, send_sem=send, recv_sem=recv, device_id=target, device_id_type=MESH
        )
        if cond is None:
            copy.start()
        else:
            pl.when(cond)(copy.start)
        started.append((cond, copy))
        return copy

    parts = 4

    def part(kind, j, h):
        return tiles[kind % 2].at[kind // 2, pl.ds(j * pieces + h * (pieces // parts), pieces // parts)]

    def arrived(e, kind, j):
        sem = row_recv.at[e, j] if kind == 0 else col_recv.at[e, j, 0]
        there = slot(2 * kind + e, j)
        pltpu.make_async_copy(there, there, sem).wait()

    def spread(e, n, j, target):
        remote(None, slot(e, j), slot(e, j), row_send.at[e, n], row_recv.at[e, j], target)

    def own(e):
        spread(e, 0, me, device(zl_=other))
        spread(e, 1, me, device(y_=(y + 1) % 4))
        spread(e, 2, me, device(y_=(y + 3) % 4))

    def cross(e):
        arrived(e, 0, across)
        spread(e, 3, across, device(y_=(y + 1) % 4))
        spread(e, 4, across, device(y_=(y + 3) % 4))

    def relay(e, near):
        side = zl if near else other
        down = ((y + 3) % 4) * 2 + side
        up = ((y + 1) % 4) * 2 + side
        arrived(e, 0, down)
        arrived(e, 0, up)
        spread(
            e, 5 if near else 6, ((y + 3 + 2 * side) % 4) * 2 + side, device(y_=(y + 1 + 2 * side) % 4)
        )

    in_flight = {True: [], False: []}

    def feed(e, j, near):
        side = zl if near else other
        queue = in_flight[near]
        for h in range(parts):
            for near_zl, lag in enumerate((4, 2)):
                if len(queue) >= lag:
                    pl.when(jnp.logical_and(is_source, zl == near_zl))(queue[-lag].wait_send)
            copy = pltpu.make_async_remote_copy(
                src_ref=part(e, j, h), dst_ref=part(2 + e, j, h), send_sem=chain_send.at[e, j, h],
                recv_sem=col_recv.at[e, j, h], device_id=device(zh_=(zh + 1 + 2 * side) % 4, core_=side),
                device_id_type=MESH,
            )
            pl.when(is_source)(copy.start)
            queue.append(copy)
        remote(
            is_source, slot(e, j), slot(2 + e, j), twin_send.at[e, j], col_recv.at[e, j, 0], device(core_=1 - core)
        )

    def feed_from(e, dy, near):
        j = ((y + dy) % 4) * 2 + (zl if near else other)
        if dy == 2:
            pl.when(is_source)(lambda: arrived(e, 0, j))
        feed(e, j, near)

    def pass_chain(e, dy):
        j = ((y + dy) % 4) * 2 + core
        for h in range(parts):
            here = part(2 + e, j, h)
            pl.when(chained)(pltpu.make_async_copy(here, here, col_recv.at[e, j, h]).wait)
            remote(onward, here, here, chain_send.at[e, j, h], col_recv.at[e, j, h], device(zh_=next_zh))
        here = slot(2 + e, j)
        remote(chained, here, here, twin_send.at[e, j], col_recv.at[e, j, 0], device(core_=1 - core))

    tell = pltpu.make_async_remote_copy(
        src_ref=map_any, dst_ref=far_v, send_sem=map_sems.at[0], recv_sem=map_sems.at[1],
        device_id=device(f=partner), device_id_type=MESH,
    )
    tell.start()
    exchange = pltpu.make_async_remote_copy(
        src_ref=slot(0, me), dst_ref=slot(1, me), send_sem=x_sem, recv_sem=row_recv.at[1, me],
        device_id=device(f=partner), device_id_type=MESH,
    )
    exchange.start()
    fronts = []
    for i in range(half):
        fronts.append(pltpu.make_async_remote_copy(
            src_ref=sent.at[i], dst_ref=came.at[i], send_sem=front_send.at[i],
            recv_sem=front_recv.at[i], device_id=device(f=partner), device_id_type=MESH,
        ))
        fronts[i].start()

    own(0)
    feed_from(0, 0, True)
    cross(0)
    feed_from(0, 0, False)
    relay(0, True)
    feed_from(0, 3, True)
    arrived(1, 0, me)
    own(1)
    relay(0, False)
    feed_from(0, 3, False)
    pass_chain(0, 0)
    feed_from(0, 1, True)
    feed_from(0, 1, False)
    cross(1)
    feed_from(0, 2, True)
    pass_chain(0, 3)
    feed_from(0, 2, False)
    relay(1, True)
    feed_from(1, 0, True)
    pass_chain(0, 1)
    feed_from(1, 0, False)
    pass_chain(0, 2)
    relay(1, False)
    for dy in (3, 1, 2):
        feed_from(1, dy, True)
        feed_from(1, dy, False)
    for dy in (0, 3, 1, 2):
        pass_chain(1, dy)

    tell.wait()
    far_copy = pltpu.make_async_copy(far_v, far_map, far_sem)
    far_copy.start()
    far_copy.wait()
    exchange.wait_send()
    loads[2].wait()
    col_kind = jnp.where(is_source, 0, 1)
    contract = (((1,), (1,)), ((), ()))

    def take(e, kind, block):
        return jnp.concatenate([tiles[e][kind, block * per_block + q] for q in range(per_block)], axis=0)

    def products(e, maps, use):
        for a in range(half):
            block = local_source(maps, row_first, parity * half + a, per_tile)
            rows = take(e, 0, block)
            for b in range(per_tile):
                source = local_source(maps, col_first, b, per_tile)
                cols = take(e, col_kind, source)
                use(a, b, block, source, lax.dot_general(rows, cols, contract, preferred_element_type=jnp.float32))

    def use_own(a, b, block, source, product):
        entries = front_v[block, source]
        mine = (entries.astype(jnp.float32) - product).astype(jnp.bfloat16).astype(jnp.float32)
        base[a, :, b * BLK:(b + 1) * BLK] = parent_v[a, :, b * BLK:(b + 1) * BLK].astype(jnp.float32) + mine

    def use_far(a, b, block, source, product):
        where = slice(b * BLK, (b + 1) * BLK)
        theirs = (came[a, b].astype(jnp.float32) - product).astype(jnp.bfloat16)
        base[a, :, where] = base[a, :, where] + theirs.astype(jnp.float32)

    def settle(e):
        for j in range(8):
            pl.when(is_twin)(lambda: arrived(e, 1, jnp.int32(j)))
        for dy in range(4):
            pl.when(chained)(lambda: arrived(e, 1, ((y + dy) % 4) * 2 + (1 - core)))
        for side in range(2):
            pl.when(jnp.logical_not(is_source))(lambda: arrived(e, 0, ((y + 2) % 4) * 2 + side))

    settle(0)
    products(0, map_ref, use_own)
    for copy in fronts:
        copy.wait()
    settle(1)
    products(1, far_map, use_far)

    for queue in in_flight.values():
        for near_zl, lag in enumerate((4, 2)):
            for copy in queue[-lag:]:
                pl.when(jnp.logical_and(is_source, zl == near_zl))(copy.wait_send)
    for cond, copy in started:
        if cond is None:
            copy.wait_send()
        else:
            pl.when(cond)(copy.wait_send)


def shards(front, panel, inverse, fill, block_map, parent_front):
    tile = front.shape[1]
    per_tile = tile // BLK
    half = per_tile // 2
    local_rows, depth = panel.shape[1:]
    anywhere = pl.BlockSpec(memory_space=pl.ANY)
    dma = pltpu.SemaphoreType.DMA
    bf16, f32 = jnp.bfloat16, jnp.float32
    factor, parent = pl.pallas_call(
        kernel,
        out_shape=(
            jax.ShapeDtypeStruct((local_rows, depth), bf16),
            pltpu.VMEM((half, BLK, tile), f32),
        ),
        in_specs=[pl.BlockSpec(memory_space=pltpu.SMEM)] * 2 + [anywhere] * 5,
        out_specs=(pl.BlockSpec(memory_space=pltpu.VMEM), pl.BlockSpec(memory_space=pltpu.VMEM)),
        scratch_shapes=[
            pltpu.VMEM((2, tile // 16, 16, depth), bf16),
            pltpu.VMEM((2, tile // 16, 16, depth), bf16),
            pltpu.VMEM((per_tile, per_tile, BLK, BLK), bf16),
            pltpu.VMEM((half, per_tile, BLK, BLK), bf16),
            pltpu.VMEM((half, per_tile, BLK, BLK), bf16),
            pltpu.VMEM((half, BLK, tile), bf16),
            pltpu.VMEM((local_rows, depth), bf16),
            pltpu.VMEM((depth, depth), bf16),
            pltpu.VMEM(block_map.shape, jnp.int32),
            pltpu.SMEM(block_map.shape, jnp.int32),
            dma((3 + per_tile,)), dma, dma((2,)), dma, dma((half,)), dma((half,)),
            dma((2, 8)), dma((2, 8, 4)), dma((2, 7)), dma((2, 8, 4)), dma((2, 8)),
        ],
        compiler_params=pltpu.CompilerParams(
            collective_id=0, has_side_effects=True, vmem_limit_bytes=56 * 2**20
        ),
        name="panel_and_extend_add",
    )(
        block_map, fill, block_map, panel[0], inverse[0], front.reshape(per_tile, BLK, tile),
        parent_front.reshape(half, BLK, tile),
    )
    return (factor[None], parent.reshape(1, half * BLK, tile))


def solution(mesh):
    placed = (
        P("front", "row", "col"),
        P("front", ("row", "col"), None),
        P("front", None, None),
        P("front", None),
        P("front", None),
        P("front", "row", "col"),
    )
    return jax.shard_map(
        shards,
        mesh=mesh,
        in_specs=placed,
        out_specs=(P("front", ("row", "col"), None), P("front", "row", "col")),
        check_vma=False,
    )
```

```python
import jax
import jax.numpy as jnp
from jax import lax
from jax.experimental import pallas as pl
from jax.experimental.pallas import tpu as pltpu
from jax.sharding import PartitionSpec as P

BLK = 256
MESH = pl.DeviceIdType.MESH


def local_source(map_ref, base, target, count):
    found = jnp.int32(0)
    for i in range(count):
        found = found + jnp.where(map_ref[0, base + i] == base + target, i, 0)
    return jnp.clip(found, 0, count - 1)


def kernel(
    map_ref, fill_ref, map_any, panel_any, inverse_any, front_any, parent_any,
    factor_ref, base,
    own_tiles, far_tiles, front_v, sent, came, parent_v, panel_v, inverse_v, far_v, far_map,
    load_sem, far_sem, map_sems, x_sem, front_send, front_recv,
    row_recv, col_recv, row_send, chain_send, twin_send,
):
    front = lax.axis_index("front")
    row = lax.axis_index("row")
    col = lax.axis_index("col")
    zh, core = row // 2, row % 2
    y, zl = col // 2, col % 2
    parity = front % 2
    partner = front + 1 - 2 * parity
    per_tile = front_v.shape[0]
    half = per_tile // 2
    local_rows = panel_v.shape[0]
    tiles = (own_tiles, far_tiles)
    fine = own_tiles.shape[2]
    pieces = local_rows // fine
    per_block = BLK // fine

    def device(f=None, zh_=None, core_=None, y_=None, zl_=None):
        return {
            "front": front if f is None else f,
            "row": (zh if zh_ is None else zh_) * 2 + (core if core_ is None else core_),
            "col": (y if y_ is None else y_) * 2 + (zl if zl_ is None else zl_),
        }

    barrier = pltpu.get_barrier_semaphore()
    peers = [device(f=partner), device(zl_=1 - zl), device(core_=1 - core)]
    peers += [device(y_=(y + n) % 4) for n in (1, 3)]
    peers += [device(zh_=(zh + n) % 4, core_=k) for n in (1, 3) for k in range(2)]
    for peer in peers:
        pl.semaphore_signal(barrier, inc=1, device_id=peer, device_id_type=MESH)

    loads = [
        pltpu.make_async_copy(panel_any, panel_v, load_sem.at[0]),
        pltpu.make_async_copy(inverse_any, inverse_v, load_sem.at[1]),
        pltpu.make_async_copy(parent_any, parent_v, load_sem.at[2]),
    ] + [
        pltpu.make_async_copy(front_any.at[:, :, pl.ds(b * BLK, BLK)], front_v.at[:, b], load_sem.at[3 + b])
        for b in range(per_tile)
    ]
    for load in loads:
        load.start()

    at_home = zh == y
    is_source = jnp.logical_and(at_home, core == zl)
    is_twin = jnp.logical_and(at_home, core != zl)
    chained = jnp.logical_not(at_home)
    distance = (zh - y + 4 + core * 2 * (y - zh)) % 4
    onward = jnp.logical_and(chained, distance < 3)
    next_zh = (zh + 1 + 2 * core) % 4
    other = 1 - zl
    me = y * 2 + zl
    across = y * 2 + other

    def slot(kind, j):
        return tiles[kind % 2].at[kind // 2, pl.ds(j * pieces, pieces)]

    loads[0].wait()
    loads[1].wait()
    size = inverse_v.shape[0]
    upper = lax.broadcasted_iota(jnp.int32, (size, size), 0) <= lax.broadcasted_iota(
        jnp.int32, (size, size), 1
    )
    inverse = jnp.where(upper, inverse_v[...].astype(jnp.float32), 0.0).astype(jnp.bfloat16)
    piece = 64
    shard = row * lax.axis_size("col") + col
    for t in range(local_rows // piece):
        block = (shard * local_rows + t * piece) // BLK
        keep = fill_ref[0, block].astype(jnp.float32)
        masked = (panel_v[t * piece:(t + 1) * piece, :].astype(jnp.float32) * keep).astype(jnp.bfloat16)
        rows = jnp.dot(masked, inverse, preferred_element_type=jnp.float32).astype(jnp.bfloat16)
        factor_ref[t * piece:(t + 1) * piece, :] = rows
        for q in range(piece // fine):
            own_tiles[0, me * pieces + t * (piece // fine) + q] = rows[q * fine:(q + 1) * fine]

    row_first = row * per_tile
    col_first = col * per_tile
    for load in loads[3:]:
        load.wait()
    for i in range(half):
        block = local_source(map_ref, row_first, (1 - parity) * half + i, per_tile)
        for b in range(per_tile):
            sent[i, b] = front_v[block, local_source(map_ref, col_first, b, per_tile)]

    pl.semaphore_wait(barrier, len(peers))

    started = []

    def remote(cond, src, dst, send, recv, target):
        copy = pltpu.make_async_remote_copy(
            src_ref=src, dst_ref=dst, send_sem=send, recv_sem=recv, device_id=target, device_id_type=MESH
        )
        if cond is None:
            copy.start()
        else:
            pl.when(cond)(copy.start)
        started.append((cond, copy))
        return copy

    parts = 4

    def part(kind, j, h):
        return tiles[kind % 2].at[kind // 2, pl.ds(j * pieces + h * (pieces // parts), pieces // parts)]

    def arrived(e, kind, j):
        sem = row_recv.at[e, j] if kind == 0 else col_recv.at[e, j, 0]
        there = slot(2 * kind + e, j)
        pltpu.make_async_copy(there, there, sem).wait()

    def spread(e, n, j, target):
        remote(None, slot(e, j), slot(e, j), row_send.at[e, n], row_recv.at[e, j], target)

    def own(e):
        spread(e, 0, me, device(zl_=other))
        spread(e, 1, me, device(y_=(y + 1) % 4))
        spread(e, 2, me, device(y_=(y + 3) % 4))

    def cross(e):
        arrived(e, 0, across)
        spread(e, 3, across, device(y_=(y + 1) % 4))
        spread(e, 4, across, device(y_=(y + 3) % 4))

    def relay(e, near):
        side = zl if near else other
        down = ((y + 3) % 4) * 2 + side
        up = ((y + 1) % 4) * 2 + side
        arrived(e, 0, down)
        arrived(e, 0, up)
        spread(
            e, 5 if near else 6, ((y + 3 + 2 * side) % 4) * 2 + side, device(y_=(y + 1 + 2 * side) % 4)
        )

    in_flight = {True: [], False: []}

    def feed(e, j, near):
        side = zl if near else other
        queue = in_flight[near]
        for h in range(parts):
            for near_zl, lag in enumerate((4, 2)):
                if len(queue) >= lag:
                    pl.when(jnp.logical_and(is_source, zl == near_zl))(queue[-lag].wait_send)
            copy = pltpu.make_async_remote_copy(
                src_ref=part(e, j, h), dst_ref=part(2 + e, j, h), send_sem=chain_send.at[e, j, h],
                recv_sem=col_recv.at[e, j, h], device_id=device(zh_=(zh + 1 + 2 * side) % 4, core_=side),
                device_id_type=MESH,
            )
            pl.when(is_source)(copy.start)
            queue.append(copy)
        remote(
            is_source, slot(e, j), slot(2 + e, j), twin_send.at[e, j], col_recv.at[e, j, 0], device(core_=1 - core)
        )

    def feed_from(e, dy, near):
        j = ((y + dy) % 4) * 2 + (zl if near else other)
        if dy == 2:
            pl.when(is_source)(lambda: arrived(e, 0, j))
        feed(e, j, near)

    def pass_chain(e, dy, among=None):
        here_on = chained if among is None else jnp.logical_and(chained, among)
        then_on = jnp.logical_and(here_on, distance < 3)
        j = ((y + dy) % 4) * 2 + core
        for h in range(parts):
            here = part(2 + e, j, h)
            pl.when(here_on)(pltpu.make_async_copy(here, here, col_recv.at[e, j, h]).wait)
            remote(then_on, here, here, chain_send.at[e, j, h], col_recv.at[e, j, h], device(zh_=next_zh))
        here = slot(2 + e, j)
        remote(here_on, here, here, twin_send.at[e, j], col_recv.at[e, j, 0], device(core_=1 - core))

    tell = pltpu.make_async_remote_copy(
        src_ref=map_any, dst_ref=far_v, send_sem=map_sems.at[0], recv_sem=map_sems.at[1],
        device_id=device(f=partner), device_id_type=MESH,
    )
    tell.start()
    exchange = pltpu.make_async_remote_copy(
        src_ref=slot(0, me), dst_ref=slot(1, me), send_sem=x_sem, recv_sem=row_recv.at[1, me],
        device_id=device(f=partner), device_id_type=MESH,
    )
    exchange.start()
    fronts = []
    for i in range(half):
        fronts.append(pltpu.make_async_remote_copy(
            src_ref=sent.at[i], dst_ref=came.at[i], send_sem=front_send.at[i],
            recv_sem=front_recv.at[i], device_id=device(f=partner), device_id_type=MESH,
        ))
        fronts[i].start()

    own(0)
    feed_from(0, 0, True)
    cross(0)
    feed_from(0, 0, False)
    relay(0, True)
    feed_from(0, 3, True)
    arrived(1, 0, me)
    own(1)
    relay(0, False)
    feed_from(0, 3, False)
    close = distance == 1
    apart = distance > 1
    pass_chain(0, 0, close)
    feed_from(0, 1, True)
    feed_from(0, 1, False)
    cross(1)
    pass_chain(0, 0, apart)
    feed_from(0, 2, True)
    pass_chain(0, 3, close)
    feed_from(0, 2, False)
    relay(1, True)
    pass_chain(0, 3, apart)
    feed_from(1, 0, True)
    pass_chain(0, 1, close)
    feed_from(1, 0, False)
    pass_chain(0, 2, close)
    relay(1, False)
    pass_chain(0, 1, apart)
    pass_chain(0, 2, apart)
    for dy in (3, 1, 2):
        feed_from(1, dy, True)
        feed_from(1, dy, False)
    for dy in (0, 3, 1, 2):
        pass_chain(1, dy)

    tell.wait()
    far_copy = pltpu.make_async_copy(far_v, far_map, far_sem)
    far_copy.start()
    far_copy.wait()
    exchange.wait_send()
    loads[2].wait()
    col_kind = jnp.where(is_source, 0, 1)
    contract = (((1,), (1,)), ((), ()))

    def take(e, kind, block):
        return jnp.concatenate([tiles[e][kind, block * per_block + q] for q in range(per_block)], axis=0)

    def products(e, maps, use):
        for a in range(half):
            block = local_source(maps, row_first, parity * half + a, per_tile)
            rows = take(e, 0, block)
            for b in range(per_tile):
                source = local_source(maps, col_first, b, per_tile)
                cols = take(e, col_kind, source)
                use(a, b, block, source, lax.dot_general(rows, cols, contract, preferred_element_type=jnp.float32))

    def use_own(a, b, block, source, product):
        entries = front_v[block, source]
        mine = (entries.astype(jnp.float32) - product).astype(jnp.bfloat16).astype(jnp.float32)
        base[a, :, b * BLK:(b + 1) * BLK] = parent_v[a, :, b * BLK:(b + 1) * BLK].astype(jnp.float32) + mine

    def use_far(a, b, block, source, product):
        where = slice(b * BLK, (b + 1) * BLK)
        theirs = (came[a, b].astype(jnp.float32) - product).astype(jnp.bfloat16)
        base[a, :, where] = base[a, :, where] + theirs.astype(jnp.float32)

    def settle(e):
        for j in range(8):
            pl.when(is_twin)(lambda: arrived(e, 1, jnp.int32(j)))
        for dy in range(4):
            pl.when(chained)(lambda: arrived(e, 1, ((y + dy) % 4) * 2 + (1 - core)))
        for side in range(2):
            pl.when(jnp.logical_not(is_source))(lambda: arrived(e, 0, ((y + 2) % 4) * 2 + side))

    settle(0)
    products(0, map_ref, use_own)
    for copy in fronts:
        copy.wait()
    settle(1)
    products(1, far_map, use_far)

    for queue in in_flight.values():
        for near_zl, lag in enumerate((4, 2)):
            for copy in queue[-lag:]:
                pl.when(jnp.logical_and(is_source, zl == near_zl))(copy.wait_send)
    for cond, copy in started:
        if cond is None:
            copy.wait_send()
        else:
            pl.when(cond)(copy.wait_send)


def shards(front, panel, inverse, fill, block_map, parent_front):
    tile = front.shape[1]
    per_tile = tile // BLK
    half = per_tile // 2
    local_rows, depth = panel.shape[1:]
    anywhere = pl.BlockSpec(memory_space=pl.ANY)
    dma = pltpu.SemaphoreType.DMA
    bf16, f32 = jnp.bfloat16, jnp.float32
    factor, parent = pl.pallas_call(
        kernel,
        out_shape=(
            jax.ShapeDtypeStruct((local_rows, depth), bf16),
            pltpu.VMEM((half, BLK, tile), f32),
        ),
        in_specs=[pl.BlockSpec(memory_space=pltpu.SMEM)] * 2 + [anywhere] * 5,
        out_specs=(pl.BlockSpec(memory_space=pltpu.VMEM), pl.BlockSpec(memory_space=pltpu.VMEM)),
        scratch_shapes=[
            pltpu.VMEM((2, tile // 16, 16, depth), bf16),
            pltpu.VMEM((2, tile // 16, 16, depth), bf16),
            pltpu.VMEM((per_tile, per_tile, BLK, BLK), bf16),
            pltpu.VMEM((half, per_tile, BLK, BLK), bf16),
            pltpu.VMEM((half, per_tile, BLK, BLK), bf16),
            pltpu.VMEM((half, BLK, tile), bf16),
            pltpu.VMEM((local_rows, depth), bf16),
            pltpu.VMEM((depth, depth), bf16),
            pltpu.VMEM(block_map.shape, jnp.int32),
            pltpu.SMEM(block_map.shape, jnp.int32),
            dma((3 + per_tile,)), dma, dma((2,)), dma, dma((half,)), dma((half,)),
            dma((2, 8)), dma((2, 8, 4)), dma((2, 7)), dma((2, 8, 4)), dma((2, 8)),
        ],
        compiler_params=pltpu.CompilerParams(
            collective_id=0, has_side_effects=True, vmem_limit_bytes=56 * 2**20
        ),
        name="panel_and_extend_add",
    )(
        block_map, fill, block_map, panel[0], inverse[0], front.reshape(per_tile, BLK, tile),
        parent_front.reshape(half, BLK, tile),
    )
    return (factor[None], parent.reshape(1, half * BLK, tile))


def solution(mesh):
    placed = (
        P("front", "row", "col"),
        P("front", ("row", "col"), None),
        P("front", None, None),
        P("front", None),
        P("front", None),
        P("front", "row", "col"),
    )
    return jax.shard_map(
        shards,
        mesh=mesh,
        in_specs=placed,
        out_specs=(P("front", ("row", "col"), None), P("front", "row", "col")),
        check_vma=False,
    )
```
